32 devices in a mesh: ga: 2 (over x), col: 16 (over z, y, core).
Axes of the slice: x: 2, y: 2, z: 4, core: 2. Of those that a mesh axis runs over, the one named last changes fastest.
Arguments:
- cholesky: bfloat16 [1024, 1024, 512], P(('ga', 'col')), parts along dimension 0, may hold values from -0.1875 to 0.1875
- amplitudes: bfloat16 [512, 512, 512], P('ga', 'col'), parts along dimension 0, may hold values from -0.25 to 0.25
Outputs:
- ladder: float32 [512, 2, 512], P('ga', None, 'col'), parts along dimension 0
The draws below stay inside these ranges and needn't reach their ends.
There are 2 independent parts, one for each index of `ga`. The reference program is written for one: setup_inputs(seed, part) draws one part's arguments, and reference() takes and returns one part's arrays. A program takes and returns all parts, laid end to end along the dimension named above; each array names one. Nothing has to cross between parts.
All inputs are finite; a program needn't handle non-finite values.
Results may differ from the reference program's by a relative error of at most 0.0029.
Values may be sent and summed in bfloat16 or wider, within the bound.
No kernel may reach another device: no remote copies, remote signals or barrier semaphores. Data moves between devices by JAX's collectives and lax.ppermute only.
A program may use at most 128 MiB of HBM per device.

```python
import jax
import jax.numpy as jnp
from jax import lax

V = 512
NCHOL = 1024
A_WIN = 2
P_SIZE = 256


def level_of(rng, dims, split, smallest, largest):
    def one(dim, parts):
        heights = jax.random.uniform(jax.random.fold_in(jax.random.fold_in(rng, 6), dim), (parts,), jnp.float32, smallest / len(split), largest / len(split))
        return jnp.repeat(jnp.exp(heights), dims[dim] // parts).reshape((-1,) + (1,) * (len(dims) - dim - 1))

    loudness = one(*split[0])
    for cut in split[1:]:
        loudness = loudness * one(*cut)
    return loudness


def centred(key, dims, spread, limit, shards=(), kind=jnp.bfloat16):
    drawn = spread * jax.random.normal(key, dims, jnp.float32)
    if shards:
        drawn = drawn * level_of(key, dims, shards, -0.22, 0.18)
    return jnp.clip(drawn, -limit, limit).astype(kind)


def setup_inputs(seed: int = 0, part: int = 0) -> dict:
    arg_keys = jax.random.split(jax.random.key(seed), 3)
    own_keys = jax.random.split(jax.random.fold_in(arg_keys[2], part), 3)
    return {
        "cholesky": centred(own_keys[0], (V, NCHOL, V), NCHOL ** -0.5, 0.1875, ((0, 16),)),
        "amplitudes": centred(own_keys[1], (P_SIZE, V, V), V ** -0.5, 0.25, ((1, 16),)),
    }


def reference(cholesky, amplitudes):
    window = cholesky[:, :, :A_WIN].astype(jnp.float32)
    block_rows = min(64, V)

    def advance(index, running):
        offset = (index * block_rows).astype(jnp.int32)
        chol_block = lax.dynamic_slice_in_dim(cholesky, offset, block_rows, 0).astype(jnp.float32)
        amp_block = lax.dynamic_slice_in_dim(amplitudes, offset, block_rows, 1).astype(jnp.float32)
        integrals = jnp.einsum("clb,dla->acbd", chol_block, window, precision=lax.Precision.HIGHEST)
        integrals = integrals.astype(jnp.bfloat16).astype(jnp.float32)
        return running + jnp.einsum("pcd,acbd->pab", amp_block, integrals, precision=lax.Precision.HIGHEST)

    initial = jnp.zeros((P_SIZE, A_WIN, V), jnp.float32)
    return lax.fori_loop(0, V // block_rows, advance, initial)
```

```python
import functools

import jax
import jax.numpy as jnp
from jax import lax
from jax.experimental import pallas as pl
from jax.experimental.pallas import tpu as pltpu
from jax.sharding import PartitionSpec as P

A_WIN = 2
CORES = 2
LANES = 128
MIB = 1 << 20


def ring_order(chips):
    return list(range(0, chips, 2)) + list(range(1, chips, 2))[::-1]


def window_kernel(rows_ref, out_ref):
    own, depth, _ = rows_ref.shape
    lane = lax.broadcasted_iota(jnp.int32, (depth, LANES), 1)
    held = [jnp.zeros((depth, LANES), jnp.float32) for _ in range(A_WIN)]
    for row in range(own):
        moved = rows_ref[row].astype(jnp.float32)
        if row:
            moved = pltpu.roll(moved, row, 1)
        for a in range(A_WIN):
            held[a] = jnp.where(lane == row + a, moved, held[a])
    for a in range(A_WIN):
        turned = jnp.transpose(held[a])
        out_ref[a] = turned[a : a + own].astype(out_ref.dtype)


def window_of(cholesky):
    own, depth, _ = cholesky.shape
    block = min(256, depth)
    return pl.pallas_call(
        window_kernel,
        out_shape=jax.ShapeDtypeStruct((A_WIN, own, depth), cholesky.dtype),
        grid=(depth // block,),
        in_specs=[pl.BlockSpec((own, block, LANES), lambda i: (0, i, 0))],
        out_specs=pl.BlockSpec((A_WIN, own, block), lambda i: (0, 0, i)),
        cost_estimate=pl.CostEstimate(flops=0, bytes_accessed=2 * own * depth * LANES, transcendentals=0),
        name="window",
    )(cholesky)


def ladder_kernel(order_ref, *refs, pieces, per_step):
    piece_refs = refs[:pieces]
    amp_ref, chol_ref, keep_ref, send_ref, window, half, total = refs[pieces:]
    step = pl.program_id(0)
    own = piece_refs[0].shape[1]
    pairs = amp_ref.shape[1]

    @pl.when(step == 0)
    def _():
        for i in range(pieces):
            start = pl.multiple_of(order_ref[i] * own, own)
            for a in range(A_WIN):
                window[a, pl.ds(start, own), :] = piece_refs[i][a]
        total[...] = jnp.zeros_like(total)

    for c in range(per_step):
        for a in range(A_WIN):
            half[a * pairs : (a + 1) * pairs, :] = jnp.dot(
                amp_ref[c], window[a], preferred_element_type=jnp.float32
            ).astype(half.dtype)
        total[...] += jnp.dot(half[...], chol_ref[c], preferred_element_type=jnp.float32)

    @pl.when(step == pl.num_programs(0) - 1)
    def _():
        core = order_ref[pieces]
        chips, _, width, _ = keep_ref.shape
        for a in range(A_WIN):
            turned = jnp.transpose(total[a * pairs : (a + 1) * pairs, :])
            total_t = turned.reshape(chips, CORES, width, pairs)
            first, second = total_t[:, 0], total_t[:, 1]
            keep_ref[:, a] = jnp.where(core == 0, first, second)
            send_ref[:, a] = jnp.where(core == 0, second, first)


def ladder_of(order, pieces, amplitudes, cholesky, chips):
    steps, pairs, orbitals = amplitudes.shape
    _, depth, _ = cholesky.shape
    own = pieces[0].shape[1]
    per_step = min(4, steps)
    width = orbitals // (chips * CORES)
    shape = jax.ShapeDtypeStruct((chips, A_WIN, width, pairs), jnp.float32)
    whole = lambda *shape: pl.BlockSpec(shape, lambda i, order: (0,) * len(shape))
    piece_spec = pl.BlockSpec((A_WIN, own, depth), lambda i, order: (0, 0, 0), pipeline_mode=pl.Buffered(1))
    flops = 2 * steps * pairs * A_WIN * orbitals * depth * 2
    return pl.pallas_call(
        functools.partial(ladder_kernel, pieces=len(pieces), per_step=per_step),
        out_shape=(shape, shape),
        grid_spec=pltpu.PrefetchScalarGridSpec(
            num_scalar_prefetch=1,
            grid=(steps // per_step,),
            in_specs=[piece_spec] * len(pieces)
            + [
                pl.BlockSpec((per_step, pairs, orbitals), lambda i, order: (i, 0, 0)),
                pl.BlockSpec((per_step, depth, orbitals), lambda i, order: (i, 0, 0)),
            ],
            out_specs=[whole(chips, A_WIN, width, pairs)] * 2,
            scratch_shapes=[
                pltpu.VMEM((A_WIN, orbitals, depth), amplitudes.dtype),
                pltpu.VMEM((A_WIN * pairs, depth), amplitudes.dtype),
                pltpu.VMEM((A_WIN * pairs, orbitals), jnp.float32),
            ],
        ),
        cost_estimate=pl.CostEstimate(
            flops=flops, bytes_accessed=2 * (cholesky.size + amplitudes.size), transcendentals=0
        ),
        compiler_params=pltpu.CompilerParams(vmem_limit_bytes=48 * MIB),
        name="ladder",
    )(order, *pieces, amplitudes, cholesky)


def shards(cholesky, amplitudes, *, devices):
    chips = devices // CORES
    ring = ring_order(chips)
    place = [ring.index(chip) for chip in range(chips)]
    me = lax.axis_index("col")
    core = me % CORES

    def along(step):
        return [
            (ring[i] * CORES + c, ring[(i + step) % chips] * CORES + c) for i in range(chips) for c in range(CORES)
        ]

    partner = [(i, i ^ 1) for i in range(devices)]
    window = window_of(cholesky)
    depth = window.shape[2]

    mine = [(0, window)]
    ahead = back = window
    for hop in range(1, chips // 2):
        ahead = lax.ppermute(ahead, "col", along(1))
        back = lax.ppermute(back, "col", along(-1))
        mine += [(-hop, ahead), (hop, back)]
    far = lax.ppermute(ahead, "col", along(1))
    mine.append((chips // 2, far))
    theirs = [(hop, lax.ppermute(piece, "col", partner)) for hop, piece in mine]

    by_step = jnp.transpose(amplitudes, (1, 0, 2))

    at = sum(jnp.where(me // CORES == chip, place[chip], 0) for chip in range(chips))

    def owner(hop):
        where = (at + hop) % chips
        return sum(jnp.where(where == i, ring[i], 0) for i in range(chips))

    order = jnp.stack(
        [owner(hop) * CORES + core for hop, _ in mine]
        + [owner(hop) * CORES + 1 - core for hop, _ in theirs]
        + [core]
    ).astype(jnp.int32)
    pieces = [piece for _, piece in mine + theirs]
    keep, send = ladder_of(order, pieces, by_step, cholesky, chips)
    summed = keep + lax.ppermute(send, "col", partner)
    groups = [[chip * CORES + c for chip in range(chips)] for c in range(CORES)]
    parts = lax.all_to_all(summed, "col", 0, 0, tiled=True, axis_index_groups=groups)
    return jnp.transpose(parts.sum(0), (2, 0, 1))


def solution(mesh):
    in_specs = (P(("ga", "col"), None, None), P("ga", "col", None))
    out_specs = P("ga", None, "col")
    body = functools.partial(shards, devices=mesh.shape["col"])
    return jax.shard_map(body, mesh=mesh, in_specs=in_specs, out_specs=out_specs, check_vma=False)
```

```python
import functools

import jax
import jax.numpy as jnp
from jax import lax
from jax.experimental import pallas as pl
from jax.experimental.pallas import tpu as pltpu
from jax.sharding import PartitionSpec as P


A_WIN = 2
CORES = 2
LANES = 128
MIB = 1 << 20
GROUP = 8
GRANT = 48 * MIB


def ring_order(chips):
    return list(range(0, chips, 2)) + list(range(1, chips, 2))[::-1]


def window_kernel(chol_ref, out_ref, rows, pick, arrived):
    own, depth, _ = rows.shape
    chunk = depth // arrived.shape[0]
    copies = []
    for i in range(depth // chunk):
        here = pl.ds(i * chunk, chunk)
        copies.append(
            pltpu.make_async_copy(chol_ref.at[:, here, pl.ds(0, LANES)], rows.at[:, here, :], arrived.at[i])
        )
        copies[i].start()
    source = lax.broadcasted_iota(jnp.int32, (LANES, LANES), 0)
    target = lax.broadcasted_iota(jnp.int32, (LANES, LANES), 1)
    for row in range(own):
        hit = source * own + row == target
        pick[row * LANES : (row + 1) * LANES, :] = jnp.where(hit & (source < A_WIN), 1.0, 0.0).astype(pick.dtype)
    for i in range(depth // chunk):
        here = slice(i * chunk, (i + 1) * chunk)
        copies[i].wait()
        wide = jnp.concatenate([rows[row, here, :] for row in range(own)], axis=1)
        picked = jnp.dot(wide, pick[...], preferred_element_type=jnp.float32)
        turned = jnp.transpose(picked)
        for a in range(A_WIN):
            out_ref[a, :, here] = turned[a * own : (a + 1) * own].astype(out_ref.dtype)


def window_of(cholesky):
    own, depth, _ = cholesky.shape
    return pl.pallas_call(
        window_kernel,
        out_shape=jax.ShapeDtypeStruct((A_WIN, own, depth), cholesky.dtype),
        in_specs=[pl.BlockSpec(memory_space=pltpu.HBM)],
        out_specs=pl.BlockSpec(memory_space=pltpu.VMEM),
        scratch_shapes=[
            pltpu.VMEM((own, depth, LANES), cholesky.dtype),
            pltpu.VMEM((own * LANES, LANES), cholesky.dtype),
            pltpu.SemaphoreType.DMA((4,)),
        ],
        cost_estimate=pl.CostEstimate(flops=0, bytes_accessed=2 * own * depth * LANES, transcendentals=0),
        compiler_params=pltpu.CompilerParams(vmem_limit_bytes=GRANT),
        name="window",
    )(cholesky)


def turn_kernel(amp_ref, *refs, first):
    out_ref, taken, given, flat, arrived, left = refs[-6:]
    chunks, rows, tile, orbitals = taken.shape
    steps = pl.ds(first, tile)
    comes, goes = [], []
    for i in range(chunks):
        here = pl.ds(i * rows, rows)
        comes.append(pltpu.make_async_copy(amp_ref.at[here, steps, :], taken.at[i], arrived.at[i]))
        goes.append(pltpu.make_async_copy(given.at[i], out_ref.at[steps, here, :], left.at[i]))
        comes[i].start()
    for i in range(chunks):
        comes[i].wait()
        for at in range(0, orbitals, LANES):
            lanes = at // LANES
            flat[lanes] = taken[i, :, :, at : at + LANES].astype(jnp.float32).reshape(rows * tile, LANES)
            for c in range(tile):
                given[i, c, :, at : at + LANES] = flat[lanes, pl.ds(c, rows, stride=tile), :].astype(given.dtype)
        goes[i].start()
    for copy in goes:
        copy.wait()


def turn(amplitudes, part, parts, held):
    pairs, steps, orbitals = amplitudes.shape
    tile = max(steps // parts, min(8, steps))
    rows = min(64, pairs)
    chunks = pairs // rows
    if part * tile >= steps:
        return held
    extra = [] if held is None else [held]
    return pl.pallas_call(
        functools.partial(turn_kernel, first=part * tile),
        out_shape=jax.ShapeDtypeStruct((steps, pairs, orbitals), amplitudes.dtype),
        in_specs=[pl.BlockSpec(memory_space=pltpu.HBM)] * (1 + len(extra)),
        out_specs=pl.BlockSpec(memory_space=pltpu.HBM),
        scratch_shapes=[
            pltpu.VMEM((chunks, rows, tile, orbitals), amplitudes.dtype),
            pltpu.VMEM((chunks, tile, rows, orbitals), amplitudes.dtype),
            pltpu.VMEM((orbitals // LANES, rows * tile, LANES), jnp.float32),
            pltpu.SemaphoreType.DMA((chunks,)),
            pltpu.SemaphoreType.DMA((chunks,)),
        ],
        input_output_aliases={1: 0} if extra else {},
        cost_estimate=pl.CostEstimate(flops=0, bytes_accessed=4 * tile * pairs * orbitals, transcendentals=0),
        compiler_params=pltpu.CompilerParams(vmem_limit_bytes=GRANT),
        name="turn",
    )(amplitudes, *extra)


def ladder_kernel(order_ref, *refs, pieces, group):
    piece_refs = refs[:pieces]
    amp_ref, chol_ref, keep_ref, send_ref, window, amps, chols, half, total, came, amp_came, chol_came = refs[pieces:]
    own = piece_refs[0].shape[1]
    steps, pairs, _ = amp_ref.shape
    groups = steps // group

    def fetch(g, slot, c):
        at = g * group + c
        return (
            pltpu.make_async_copy(amp_ref.at[at], amps.at[slot, c], amp_came.at[slot, c]),
            pltpu.make_async_copy(chol_ref.at[at], chols.at[slot, c], chol_came.at[slot, c]),
        )

    gathered = []
    for i in range(pieces):
        start = pl.multiple_of(order_ref[i] * own, own)
        gathered.append(pltpu.make_async_copy(piece_refs[i], window.at[:, pl.ds(start, own), :], came.at[i]))
        gathered[i].start()
    for c in range(group):
        for copy in fetch(0, 0, c):
            copy.start()
    total[...] = jnp.zeros_like(total)
    for copy in gathered:
        copy.wait()

    def advance(g, _):
        slot = lax.rem(g, 2)

        @pl.when(g + 1 < groups)
        def _():
            for c in range(group):
                for copy in fetch(g + 1, 1 - slot, c):
                    copy.start()

        for c in range(group):
            for copy in fetch(g, slot, c):
                copy.wait()
            for a in range(A_WIN):
                half[c, a * pairs : (a + 1) * pairs, :] = jnp.dot(
                    amps[slot, c], window[a], preferred_element_type=jnp.float32
                ).astype(half.dtype)
            total[...] += jnp.dot(half[c], chols[slot, c], preferred_element_type=jnp.float32)
        return 0

    lax.fori_loop(0, groups, advance, 0)
    core = order_ref[pieces]
    chips, _, width, _ = keep_ref.shape
    for a in range(A_WIN):
        turned = jnp.transpose(total[a * pairs : (a + 1) * pairs, :])
        total_t = turned.reshape(chips, CORES, width, pairs)
        first, second = total_t[:, 0], total_t[:, 1]
        keep_ref[:, a] = jnp.where(core == 0, first, second)
        send_ref[:, a] = jnp.where(core == 0, second, first)


def ladder_of(order, pieces, amplitudes, cholesky, chips):
    steps, pairs, orbitals = amplitudes.shape
    _, depth, _ = cholesky.shape
    group = GROUP if steps % GROUP == 0 else 1
    width = orbitals // (chips * CORES)
    shape = jax.ShapeDtypeStruct((chips, A_WIN, width, pairs), jnp.float32)
    flops = 2 * steps * pairs * A_WIN * orbitals * depth * 2
    kind = amplitudes.dtype
    return pl.pallas_call(
        functools.partial(ladder_kernel, pieces=len(pieces), group=group),
        out_shape=(shape, shape),
        in_specs=[pl.BlockSpec(memory_space=pltpu.SMEM)]
        + [pl.BlockSpec(memory_space=pl.ANY)] * len(pieces)
        + [pl.BlockSpec(memory_space=pltpu.HBM)] * 2,
        out_specs=[pl.BlockSpec(memory_space=pltpu.VMEM)] * 2,
        scratch_shapes=[
            pltpu.VMEM((A_WIN, orbitals, depth), kind),
            pltpu.VMEM((2, group, pairs, orbitals), kind),
            pltpu.VMEM((2, group, depth, orbitals), kind),
            pltpu.VMEM((group, A_WIN * pairs, depth), kind),
            pltpu.VMEM((A_WIN * pairs, orbitals), jnp.float32),
            pltpu.SemaphoreType.DMA((len(pieces),)),
            pltpu.SemaphoreType.DMA((2, group)),
            pltpu.SemaphoreType.DMA((2, group)),
        ],
        cost_estimate=pl.CostEstimate(
            flops=flops, bytes_accessed=2 * (cholesky.size + amplitudes.size), transcendentals=0
        ),
        compiler_params=pltpu.CompilerParams(vmem_limit_bytes=GRANT),
        name="ladder",
    )(order, *pieces, amplitudes, cholesky)


def shards(cholesky, amplitudes, *, devices):
    return part(cholesky, amplitudes, devices)


def part(cholesky, amplitudes, devices):
    chips = devices // CORES
    ring = ring_order(chips)
    place = [ring.index(chip) for chip in range(chips)]
    me = lax.axis_index("col")
    core = me % CORES

    def along(step):
        return [
            (ring[i] * CORES + c, ring[(i + step) % chips] * CORES + c) for i in range(chips) for c in range(CORES)
        ]

    partner = [(i, i ^ 1) for i in range(devices)]
    window = window_of(cholesky)

    def hop(piece, step):
        return lax.ppermute(piece, "col", along(step))

    mine = [(0, window)]
    ahead = back = window
    by_step = None
    hops = chips // 2
    for at_hop in range(1, hops + 1):
        ahead = hop(ahead, 1)
        mine.append((-at_hop, ahead))
        if at_hop < hops:
            back = hop(back, -1)
            mine.append((at_hop, back))
        by_step = turn(amplitudes, at_hop - 1, hops, by_step)
    theirs = [(far, lax.ppermute(piece, "col", partner)) for far, piece in mine]

    at = sum(jnp.where(me // CORES == chip, place[chip], 0) for chip in range(chips))

    def owner(away):
        where = (at + away) % chips
        return sum(jnp.where(where == i, ring[i], 0) for i in range(chips))

    order = jnp.stack(
        [owner(far) * CORES + core for far, _ in mine]
        + [owner(far) * CORES + 1 - core for far, _ in theirs]
        + [core]
    ).astype(jnp.int32)
    pieces = [piece for _, piece in mine + theirs]
    keep, send = ladder_of(order, pieces, by_step, cholesky, chips)
    summed = keep + lax.ppermute(send, "col", partner)
    groups = [[chip * CORES + c for chip in range(chips)] for c in range(CORES)]
    parts = lax.all_to_all(summed, "col", 0, 0, tiled=True, axis_index_groups=groups)
    return jnp.transpose(parts.sum(0), (2, 0, 1))


def solution(mesh):
    in_specs = (P(("ga", "col"), None, None), P("ga", "col", None))
    out_specs = P("ga", None, "col")
    devices = mesh.shape["col"]
    body = functools.partial(shards, devices=devices)
    return jax.shard_map(body, mesh=mesh, in_specs=in_specs, out_specs=out_specs, check_vma=False)
```

```python
import functools

import jax
import jax.numpy as jnp
from jax import lax
from jax.experimental import pallas as pl
from jax.experimental.pallas import tpu as pltpu
from jax.sharding import PartitionSpec as P


A_WIN = 2
CORES = 2
LANES = 128
MIB = 1 << 20
GROUP = 32
SLOTS = 4
GRANT = 48 * MIB


def ring_order(chips):
    return list(range(0, chips, 2)) + list(range(1, chips, 2))[::-1]


def window_kernel(chol_ref, out_ref, rows, pick, arrived):
    own, depth, _ = rows.shape
    chunk = depth // arrived.shape[0]
    copies = []
    for i in range(depth // chunk):
        here = pl.ds(i * chunk, chunk)
        copies.append(
            pltpu.make_async_copy(chol_ref.at[:, here, pl.ds(0, LANES)], rows.at[:, here, :], arrived.at[i])
        )
        copies[i].start()
    source = lax.broadcasted_iota(jnp.int32, (LANES, LANES), 0)
    target = lax.broadcasted_iota(jnp.int32, (LANES, LANES), 1)
    for row in range(own):
        hit = source * own + row == target
        pick[row * LANES : (row + 1) * LANES, :] = jnp.where(hit & (source < A_WIN), 1.0, 0.0).astype(pick.dtype)
    for i in range(depth // chunk):
        here = slice(i * chunk, (i + 1) * chunk)
        copies[i].wait()
        wide = jnp.concatenate([rows[row, here, :] for row in range(own)], axis=1)
        picked = jnp.dot(wide, pick[...], preferred_element_type=jnp.float32)
        turned = jnp.transpose(picked)
        for a in range(A_WIN):
            out_ref[a, :, here] = turned[a * own : (a + 1) * own].astype(out_ref.dtype)


def window_of(cholesky):
    own, depth, _ = cholesky.shape
    return pl.pallas_call(
        window_kernel,
        out_shape=jax.ShapeDtypeStruct((A_WIN, own, depth), cholesky.dtype),
        in_specs=[pl.BlockSpec(memory_space=pltpu.HBM)],
        out_specs=pl.BlockSpec(memory_space=pltpu.VMEM),
        scratch_shapes=[
            pltpu.VMEM((own, depth, LANES), cholesky.dtype),
            pltpu.VMEM((own * LANES, LANES), cholesky.dtype),
            pltpu.SemaphoreType.DMA((4,)),
        ],
        cost_estimate=pl.CostEstimate(flops=0, bytes_accessed=2 * own * depth * LANES, transcendentals=0),
        compiler_params=pltpu.CompilerParams(vmem_limit_bytes=GRANT),
        name="window",
    )(cholesky)


def turn_kernel(amp_ref, *refs, first):
    out_ref, taken, given, flat, arrived, left = refs[-6:]
    chunks, rows, tile, orbitals = taken.shape
    steps = pl.ds(first, tile)
    comes, goes = [], []
    for i in range(chunks):
        here = pl.ds(i * rows, rows)
        comes.append(pltpu.make_async_copy(amp_ref.at[here, steps, :], taken.at[i], arrived.at[i]))
        goes.append(pltpu.make_async_copy(given.at[i], out_ref.at[steps, here, :], left.at[i]))
        comes[i].start()
    for i in range(chunks):
        comes[i].wait()
        for at in range(0, orbitals, LANES):
            lanes = at // LANES
            flat[lanes] = taken[i, :, :, at : at + LANES].astype(jnp.float32).reshape(rows * tile, LANES)
            for c in range(tile):
                given[i, c, :, at : at + LANES] = flat[lanes, pl.ds(c, rows, stride=tile), :].astype(given.dtype)
        goes[i].start()
    for copy in goes:
        copy.wait()


def turn(amplitudes, part, parts, held):
    pairs, steps, orbitals = amplitudes.shape
    tile = max(steps // parts, min(8, steps))
    rows = min(32, pairs)
    chunks = pairs // rows
    if part * tile >= steps:
        return held
    extra = [] if held is None else [held]
    return pl.pallas_call(
        functools.partial(turn_kernel, first=part * tile),
        out_shape=jax.ShapeDtypeStruct((steps, pairs, orbitals), amplitudes.dtype),
        in_specs=[pl.BlockSpec(memory_space=pltpu.HBM)] * (1 + len(extra)),
        out_specs=pl.BlockSpec(memory_space=pltpu.HBM),
        scratch_shapes=[
            pltpu.VMEM((chunks, rows, tile, orbitals), amplitudes.dtype),
            pltpu.VMEM((chunks, tile, rows, orbitals), amplitudes.dtype),
            pltpu.VMEM((orbitals // LANES, rows * tile, LANES), jnp.float32),
            pltpu.SemaphoreType.DMA((chunks,)),
            pltpu.SemaphoreType.DMA((chunks,)),
        ],
        input_output_aliases={1: 0} if extra else {},
        cost_estimate=pl.CostEstimate(flops=0, bytes_accessed=4 * tile * pairs * orbitals, transcendentals=0),
        compiler_params=pltpu.CompilerParams(vmem_limit_bytes=GRANT),
        name="turn",
    )(amplitudes, *extra)


def ladder_kernel(order_ref, *refs, pieces, group, slots):
    piece_refs = refs[:pieces]
    amp_ref, chol_ref, keep_ref, send_ref, window, amps, chols, half, total, amp_came, chol_came = refs[pieces:]
    own = piece_refs[0].shape[1]
    steps, pairs, _ = amp_ref.shape
    groups = steps // group

    def fetch(at, slot):
        return (
            pltpu.make_async_copy(amp_ref.at[at], amps.at[slot], amp_came.at[slot]),
            pltpu.make_async_copy(chol_ref.at[at], chols.at[slot], chol_came.at[slot]),
        )

    for c in range(2):
        for copy in fetch(c, c):
            copy.start()
    for c in range(2, slots - 1):
        for copy in fetch(c, c):
            copy.start()
    total[...] = jnp.zeros_like(total)
    for i in range(pieces):
        start = pl.multiple_of(order_ref[i] * own, own)
        for a in range(A_WIN):
            window[a, pl.ds(start, own), :] = piece_refs[i][a]

    def advance(g, _):
        for u in range(group):
            at = g * group + u
            slot, spare = u % slots, (u - 1) % slots
            for copy in fetch(at, slot):
                copy.wait()

            @pl.when(at + slots - 1 < steps)
            def _():
                for copy in fetch(at + slots - 1, spare):
                    copy.start()

            for a in range(A_WIN):
                half[u % 2, a * pairs : (a + 1) * pairs, :] = jnp.dot(
                    amps[slot], window[a], preferred_element_type=jnp.float32
                ).astype(half.dtype)
            total[...] += jnp.dot(half[u % 2], chols[slot], preferred_element_type=jnp.float32)
        return 0

    lax.fori_loop(0, groups, advance, 0)
    core = order_ref[pieces]
    chips, _, width, _ = keep_ref.shape
    for a in range(A_WIN):
        turned = jnp.transpose(total[a * pairs : (a + 1) * pairs, :])
        total_t = turned.reshape(chips, CORES, width, pairs)
        first, second = total_t[:, 0], total_t[:, 1]
        keep_ref[:, a] = jnp.where(core == 0, first, second)
        send_ref[:, a] = jnp.where(core == 0, second, first)


def ladder_of(order, pieces, amplitudes, cholesky, chips):
    steps, pairs, orbitals = amplitudes.shape
    _, depth, _ = cholesky.shape
    group = GROUP if steps % GROUP == 0 else 1
    slots = min(SLOTS, group)
    width = orbitals // (chips * CORES)
    shape = jax.ShapeDtypeStruct((chips, A_WIN, width, pairs), jnp.float32)
    flops = 2 * steps * pairs * A_WIN * orbitals * depth * 2
    kind = amplitudes.dtype
    return pl.pallas_call(
        functools.partial(ladder_kernel, pieces=len(pieces), group=group, slots=slots),
        out_shape=(shape, shape),
        in_specs=[pl.BlockSpec(memory_space=pltpu.SMEM)]
        + [pl.BlockSpec(memory_space=pltpu.VMEM)] * len(pieces)
        + [pl.BlockSpec(memory_space=pltpu.HBM)] * 2,
        out_specs=[pl.BlockSpec(memory_space=pltpu.VMEM)] * 2,
        scratch_shapes=[
            pltpu.VMEM((A_WIN, orbitals, depth), kind),
            pltpu.VMEM((slots, pairs, orbitals), kind),
            pltpu.VMEM((slots, depth, orbitals), kind),
            pltpu.VMEM((2, A_WIN * pairs, depth), kind),
            pltpu.VMEM((A_WIN * pairs, orbitals), jnp.float32),
            pltpu.SemaphoreType.DMA((slots,)),
            pltpu.SemaphoreType.DMA((slots,)),
        ],
        cost_estimate=pl.CostEstimate(
            flops=flops, bytes_accessed=2 * (cholesky.size + amplitudes.size), transcendentals=0
        ),
        compiler_params=pltpu.CompilerParams(vmem_limit_bytes=GRANT),
        name="ladder",
    )(order, *pieces, amplitudes, cholesky)


def shards(cholesky, amplitudes, *, devices):
    return part(cholesky, amplitudes, devices)


def part(cholesky, amplitudes, devices):
    chips = devices // CORES
    ring = ring_order(chips)
    place = [ring.index(chip) for chip in range(chips)]
    me = lax.axis_index("col")
    core = me % CORES

    def along(step):
        return [
            (ring[i] * CORES + c, ring[(i + step) % chips] * CORES + c) for i in range(chips) for c in range(CORES)
        ]

    partner = [(i, i ^ 1) for i in range(devices)]
    window = window_of(cholesky)

    def hop(piece, step):
        return lax.ppermute(piece, "col", along(step))

    mine = [(0, window)]
    ahead = back = window
    by_step = None
    hops = chips // 2
    for at_hop in range(1, hops + 1):
        ahead = hop(ahead, 1)
        mine.append((-at_hop, ahead))
        if at_hop < hops:
            back = hop(back, -1)
            mine.append((at_hop, back))
        by_step = turn(amplitudes, at_hop - 1, hops, by_step)
    theirs = [(far, lax.ppermute(piece, "col", partner)) for far, piece in mine]

    at = sum(jnp.where(me // CORES == chip, place[chip], 0) for chip in range(chips))

    def owner(away):
        where = (at + away) % chips
        return sum(jnp.where(where == i, ring[i], 0) for i in range(chips))

    order = jnp.stack(
        [owner(far) * CORES + core for far, _ in mine]
        + [owner(far) * CORES + 1 - core for far, _ in theirs]
        + [core]
    ).astype(jnp.int32)
    pieces = [piece for _, piece in mine + theirs]
    keep, send = ladder_of(order, pieces, by_step, cholesky, chips)
    summed = keep + lax.ppermute(send, "col", partner)
    groups = [[chip * CORES + c for chip in range(chips)] for c in range(CORES)]
    parts = lax.all_to_all(summed.astype(jnp.bfloat16), "col", 0, 0, tiled=True, axis_index_groups=groups)
    mine_at = lax.broadcasted_iota(jnp.int32, (chips, 1, 1, 1), 0) == me // CORES
    ladder = jnp.where(mine_at, summed, parts.astype(jnp.float32)).sum(0)
    return jnp.transpose(ladder, (2, 0, 1))


def solution(mesh):
    in_specs = (P(("ga", "col"), None, None), P("ga", "col", None))
    out_specs = P("ga", None, "col")
    devices = mesh.shape["col"]
    body = functools.partial(shards, devices=devices)
    return jax.shard_map(body, mesh=mesh, in_specs=in_specs, out_specs=out_specs, check_vma=False)
```

```python
import functools

import jax
import jax.numpy as jnp
from jax import lax
from jax.experimental import pallas as pl
from jax.experimental.pallas import tpu as pltpu
from jax.sharding import PartitionSpec as P


A_WIN = 2
CORES = 2
LANES = 128
MIB = 1 << 20
GROUP = 8
SLOTS = 16
GRANT = 48 * MIB


def ring_order(chips):
    return list(range(0, chips, 2)) + list(range(1, chips, 2))[::-1]


def window_kernel(chol_ref, out_ref, rows, pick, arrived):
    own, depth, _ = rows.shape
    chunk = depth // arrived.shape[0]
    copies = []
    for i in range(depth // chunk):
        here = pl.ds(i * chunk, chunk)
        copies.append(
            pltpu.make_async_copy(chol_ref.at[:, here, pl.ds(0, LANES)], rows.at[:, here, :], arrived.at[i])
        )
        copies[i].start()
    source = lax.broadcasted_iota(jnp.int32, (LANES, LANES), 0)
    target = lax.broadcasted_iota(jnp.int32, (LANES, LANES), 1)
    upper = own // 2
    for row in range(upper):
        low = (source < A_WIN) & (source * own + row == target)
        high = (source >= A_WIN) & (source < 2 * A_WIN) & ((source - A_WIN) * own + upper + row == target)
        pick[row * LANES : (row + 1) * LANES, :] = jnp.where(low | high, 1.0, 0.0).astype(pick.dtype)
    first = lax.broadcasted_iota(jnp.int32, (chunk, LANES), 1) < A_WIN

    def joined(row, here):
        moved = pltpu.roll(rows[upper + row, here, :].astype(jnp.float32), A_WIN, 1)
        return jnp.where(first, rows[row, here, :].astype(jnp.float32), moved).astype(pick.dtype)

    for i in range(depth // chunk):
        here = slice(i * chunk, (i + 1) * chunk)
        copies[i].wait()
        wide = jnp.concatenate([joined(row, here) for row in range(upper)], axis=1)
        picked = jnp.dot(wide, pick[...], preferred_element_type=jnp.float32)
        turned = jnp.transpose(picked)
        for a in range(A_WIN):
            out_ref[a, :, here] = turned[a * own : (a + 1) * own].astype(out_ref.dtype)


def window_of(cholesky):
    own, depth, _ = cholesky.shape
    return pl.pallas_call(
        window_kernel,
        out_shape=jax.ShapeDtypeStruct((A_WIN, own, depth), cholesky.dtype),
        in_specs=[pl.BlockSpec(memory_space=pltpu.HBM)],
        out_specs=pl.BlockSpec(memory_space=pltpu.VMEM),
        scratch_shapes=[
            pltpu.VMEM((own, depth, LANES), cholesky.dtype),
            pltpu.VMEM((own // 2 * LANES, LANES), cholesky.dtype),
            pltpu.SemaphoreType.DMA((4,)),
        ],
        cost_estimate=pl.CostEstimate(flops=0, bytes_accessed=2 * own * depth * LANES, transcendentals=0),
        compiler_params=pltpu.CompilerParams(vmem_limit_bytes=GRANT),
        name="window",
    )(cholesky)


def turn_kernel(amp_ref, *refs, first):
    out_ref, taken, given, flat, arrived, left = refs[-6:]
    chunks, rows, tile, orbitals = taken.shape
    steps = pl.ds(first, tile)
    comes, goes = [], []
    for i in range(chunks):
        here = pl.ds(i * rows, rows)
        comes.append(pltpu.make_async_copy(amp_ref.at[here, steps, :], taken.at[i], arrived.at[i]))
        goes.append(pltpu.make_async_copy(given.at[i], out_ref.at[steps, here, :], left.at[i]))
        comes[i].start()
    for i in range(chunks):
        comes[i].wait()
        for at in range(0, orbitals, LANES):
            lanes = at // LANES
            flat[lanes, : rows * tile] = taken[i, :, :, at : at + LANES].astype(jnp.float32).reshape(rows * tile, LANES)
            for c in range(tile):
                given[i, c, :, at : at + LANES] = flat[lanes, pl.ds(c, rows, stride=tile), :].astype(given.dtype)
        goes[i].start()
    for copy in goes:
        copy.wait()


def turn(amplitudes, part, parts, held):
    pairs, steps, orbitals = amplitudes.shape
    tile = max(steps // parts, min(8, steps))
    rows = min(32, pairs)
    chunks = pairs // rows
    if part * tile >= steps:
        return held
    extra = [] if held is None else [held]
    return pl.pallas_call(
        functools.partial(turn_kernel, first=part * tile),
        out_shape=jax.ShapeDtypeStruct((steps, pairs, orbitals), amplitudes.dtype),
        in_specs=[pl.BlockSpec(memory_space=pltpu.HBM)] * (1 + len(extra)),
        out_specs=pl.BlockSpec(memory_space=pltpu.HBM),
        scratch_shapes=[
            pltpu.VMEM((chunks, rows, tile, orbitals), amplitudes.dtype),
            pltpu.VMEM((chunks, tile, rows, orbitals), amplitudes.dtype),
            pltpu.VMEM((orbitals // LANES, (rows + 1) * tile, LANES), jnp.float32),
            pltpu.SemaphoreType.DMA((chunks,)),
            pltpu.SemaphoreType.DMA((chunks,)),
        ],
        input_output_aliases={1: 0} if extra else {},
        cost_estimate=pl.CostEstimate(flops=0, bytes_accessed=4 * tile * pairs * orbitals, transcendentals=0),
        compiler_params=pltpu.CompilerParams(vmem_limit_bytes=GRANT),
        name="turn",
    )(amplitudes, *extra)


def ladder_kernel(order_ref, *refs, pieces, slots):
    piece_refs = refs[:pieces]
    amp_ref, chol_ref, keep_ref, send_ref, window, amps, chols, half, total, amp_came, chol_came = refs[pieces:]
    own = piece_refs[0].shape[1]
    steps, pairs, _ = amp_ref.shape

    def fetch(at, slot):
        return (
            pltpu.make_async_copy(amp_ref.at[at], amps.at[slot], amp_came.at[slot]),
            pltpu.make_async_copy(chol_ref.at[at], chols.at[slot], chol_came.at[slot]),
        )

    def issue(after, upto):
        for c in range(after, min(upto, steps)):
            for copy in fetch(c, c % slots):
                copy.start()
        return max(after, min(upto, steps))

    issued = issue(0, slots - 1)
    total[...] = jnp.zeros_like(total)
    for i in range(pieces):
        start = pl.multiple_of(order_ref[i] * own, own)
        for a in range(A_WIN):
            window[a, pl.ds(start, own), :] = piece_refs[i][a]

    first, size = 0, 1
    while first < steps:
        here = range(first, min(first + size, steps))
        for c in here:
            for copy in fetch(c, c % slots):
                copy.wait()
        issued = issue(issued, first + slots)
        for c in here:
            for a in range(A_WIN):
                half[c % 2, a * pairs : (a + 1) * pairs, :] = jnp.dot(
                    amps[c % slots], window[a], preferred_element_type=jnp.float32
                ).astype(half.dtype)
            total[...] += jnp.dot(half[c % 2], chols[c % slots], preferred_element_type=jnp.float32)
        first += size
        size = min(GROUP, first)

    core = order_ref[pieces]
    chips, _, width, _ = keep_ref.shape
    for a in range(A_WIN):
        turned = jnp.transpose(total[a * pairs : (a + 1) * pairs, :])
        total_t = turned.reshape(chips, CORES, width, pairs)
        first, second = total_t[:, 0], total_t[:, 1]
        keep_ref[:, a] = jnp.where(core == 0, first, second)
        send_ref[:, a] = jnp.where(core == 0, second, first)


def ladder_of(order, pieces, amplitudes, cholesky, chips):
    steps, pairs, orbitals = amplitudes.shape
    _, depth, _ = cholesky.shape
    slots = min(SLOTS, steps)
    width = orbitals // (chips * CORES)
    shape = jax.ShapeDtypeStruct((chips, A_WIN, width, pairs), jnp.float32)
    flops = 2 * steps * pairs * A_WIN * orbitals * depth * 2
    kind = amplitudes.dtype
    return pl.pallas_call(
        functools.partial(ladder_kernel, pieces=len(pieces), slots=slots),
        out_shape=(shape, shape),
        in_specs=[pl.BlockSpec(memory_space=pltpu.SMEM)]
        + [pl.BlockSpec(memory_space=pltpu.VMEM)] * len(pieces)
        + [pl.BlockSpec(memory_space=pltpu.HBM)] * 2,
        out_specs=[pl.BlockSpec(memory_space=pltpu.VMEM)] * 2,
        scratch_shapes=[
            pltpu.VMEM((A_WIN, orbitals, depth), kind),
            pltpu.VMEM((slots, pairs, orbitals), kind),
            pltpu.VMEM((slots, depth, orbitals), kind),
            pltpu.VMEM((2, A_WIN * pairs, depth), kind),
            pltpu.VMEM((A_WIN * pairs, orbitals), jnp.float32),
            pltpu.SemaphoreType.DMA((slots,)),
            pltpu.SemaphoreType.DMA((slots,)),
        ],
        cost_estimate=pl.CostEstimate(
            flops=flops, bytes_accessed=2 * (cholesky.size + amplitudes.size), transcendentals=0
        ),
        compiler_params=pltpu.CompilerParams(vmem_limit_bytes=GRANT),
        name="ladder",
    )(order, *pieces, amplitudes, cholesky)


def shards(cholesky, amplitudes, *, devices):
    return part(cholesky, amplitudes, devices)


def part(cholesky, amplitudes, devices):
    chips = devices // CORES
    ring = ring_order(chips)
    place = [ring.index(chip) for chip in range(chips)]
    me = lax.axis_index("col")
    core = me % CORES

    def along(step):
        return [
            (ring[i] * CORES + c, ring[(i + step) % chips] * CORES + c) for i in range(chips) for c in range(CORES)
        ]

    partner = [(i, i ^ 1) for i in range(devices)]
    window = window_of(cholesky)

    def hop(piece, step):
        return lax.ppermute(piece, "col", along(step))

    mine = [(0, window)]
    ahead = back = window
    by_step = None
    hops = chips // 2
    for at_hop in range(1, hops + 1):
        ahead = hop(ahead, 1)
        mine.append((-at_hop, ahead))
        if at_hop < hops:
            back = hop(back, -1)
            mine.append((at_hop, back))
        by_step = turn(amplitudes, at_hop - 1, hops, by_step)
    theirs = [(far, lax.ppermute(piece, "col", partner)) for far, piece in mine]

    at = sum(jnp.where(me // CORES == chip, place[chip], 0) for chip in range(chips))

    def owner(away):
        where = (at + away) % chips
        return sum(jnp.where(where == i, ring[i], 0) for i in range(chips))

    order = jnp.stack(
        [owner(far) * CORES + core for far, _ in mine]
        + [owner(far) * CORES + 1 - core for far, _ in theirs]
        + [core]
    ).astype(jnp.int32)
    pieces = [piece for _, piece in mine + theirs]
    keep, send = ladder_of(order, pieces, by_step, cholesky, chips)
    summed = keep + lax.ppermute(send, "col", partner)
    groups = [[chip * CORES + c for chip in range(chips)] for c in range(CORES)]
    parts = lax.all_to_all(summed.astype(jnp.bfloat16), "col", 0, 0, tiled=True, axis_index_groups=groups)
    mine_at = lax.broadcasted_iota(jnp.int32, (chips, 1, 1, 1), 0) == me // CORES
    ladder = jnp.where(mine_at, summed, parts.astype(jnp.float32)).sum(0)
    return jnp.transpose(ladder, (2, 0, 1))


def solution(mesh):
    in_specs = (P(("ga", "col"), None, None), P("ga", "col", None))
    out_specs = P("ga", None, "col")
    devices = mesh.shape["col"]
    body = functools.partial(shards, devices=devices)
    return jax.shard_map(body, mesh=mesh, in_specs=in_specs, out_specs=out_specs, check_vma=False)
```

```python
import functools

import jax
import jax.numpy as jnp
from jax import lax
from jax.experimental import pallas as pl
from jax.experimental.pallas import tpu as pltpu
from jax.sharding import PartitionSpec as P


A_WIN = 2
CORES = 2
LANES = 128
MIB = 1 << 20
GROUP = 8
SLOTS = 16
GRANT = 48 * MIB


def ring_order(chips):
    return list(range(0, chips, 2)) + list(range(1, chips, 2))[::-1]


def window_kernel(chol_ref, out_ref, rows, pick, arrived):
    own, depth, _ = rows.shape
    chunk = depth // arrived.shape[0]
    copies = []
    for i in range(depth // chunk):
        here = pl.ds(i * chunk, chunk)
        copies.append(
            pltpu.make_async_copy(chol_ref.at[:, here, pl.ds(0, LANES)], rows.at[:, here, :], arrived.at[i])
        )
        copies[i].start()
    source = lax.broadcasted_iota(jnp.int32, (LANES, LANES), 0)
    target = lax.broadcasted_iota(jnp.int32, (LANES, LANES), 1)
    upper = own // 2
    for row in range(upper):
        low = (source < A_WIN) & (source * own + row == target)
        high = (source >= A_WIN) & (source < 2 * A_WIN) & ((source - A_WIN) * own + upper + row == target)
        pick[row * LANES : (row + 1) * LANES, :] = jnp.where(low | high, 1.0, 0.0).astype(pick.dtype)
    first = lax.broadcasted_iota(jnp.int32, (chunk, LANES), 1) < A_WIN

    def joined(row, here):
        moved = pltpu.roll(rows[upper + row, here, :].astype(jnp.float32), A_WIN, 1)
        return jnp.where(first, rows[row, here, :].astype(jnp.float32), moved).astype(pick.dtype)

    for i in range(depth // chunk):
        here = slice(i * chunk, (i + 1) * chunk)
        copies[i].wait()
        wide = jnp.concatenate([joined(row, here) for row in range(upper)], axis=1)
        picked = jnp.dot(wide, pick[...], preferred_element_type=jnp.float32)
        turned = jnp.transpose(picked)
        for a in range(A_WIN):
            out_ref[a, :, here] = turned[a * own : (a + 1) * own].astype(out_ref.dtype)


def window_of(cholesky):
    own, depth, _ = cholesky.shape
    return pl.pallas_call(
        window_kernel,
        out_shape=jax.ShapeDtypeStruct((A_WIN, own, depth), cholesky.dtype),
        in_specs=[pl.BlockSpec(memory_space=pltpu.HBM)],
        out_specs=pl.BlockSpec(memory_space=pltpu.VMEM),
        scratch_shapes=[
            pltpu.VMEM((own, depth, LANES), cholesky.dtype),
            pltpu.VMEM((own // 2 * LANES, LANES), cholesky.dtype),
            pltpu.SemaphoreType.DMA((4,)),
        ],
        cost_estimate=pl.CostEstimate(flops=0, bytes_accessed=2 * own * depth * LANES, transcendentals=0),
        compiler_params=pltpu.CompilerParams(vmem_limit_bytes=GRANT),
        name="window",
    )(cholesky)


def turn_kernel(amp_ref, *refs, first):
    out_ref, taken, given, flat, arrived, left = refs[-6:]
    chunks, rows, tile, orbitals = taken.shape
    steps = pl.ds(first, tile)
    comes, goes = [], []
    for i in range(chunks):
        here = pl.ds(i * rows, rows)
        comes.append(pltpu.make_async_copy(amp_ref.at[here, steps, :], taken.at[i], arrived.at[i]))
        goes.append(pltpu.make_async_copy(given.at[i], out_ref.at[steps, here, :], left.at[i]))
        comes[i].start()
    for i in range(chunks):
        comes[i].wait()
        for at in range(0, orbitals, LANES):
            lanes = at // LANES
            flat[lanes, : rows * tile] = taken[i, :, :, at : at + LANES].astype(jnp.float32).reshape(rows * tile, LANES)
            for c in range(tile):
                given[i, c, :, at : at + LANES] = flat[lanes, pl.ds(c, rows, stride=tile), :].astype(given.dtype)
        goes[i].start()
    for copy in goes:
        copy.wait()


def turn(amplitudes, part, parts, held):
    pairs, steps, orbitals = amplitudes.shape
    tile = max(steps // parts, min(8, steps))
    rows = min(32, pairs)
    chunks = pairs // rows
    if part * tile >= steps:
        return held
    extra = [] if held is None else [held]
    return pl.pallas_call(
        functools.partial(turn_kernel, first=part * tile),
        out_shape=jax.ShapeDtypeStruct((steps, pairs, orbitals), amplitudes.dtype),
        in_specs=[pl.BlockSpec(memory_space=pltpu.HBM)] * (1 + len(extra)),
        out_specs=pl.BlockSpec(memory_space=pltpu.HBM),
        scratch_shapes=[
            pltpu.VMEM((chunks, rows, tile, orbitals), amplitudes.dtype),
            pltpu.VMEM((chunks, tile, rows, orbitals), amplitudes.dtype),
            pltpu.VMEM((orbitals // LANES, (rows + 1) * tile, LANES), jnp.float32),
            pltpu.SemaphoreType.DMA((chunks,)),
            pltpu.SemaphoreType.DMA((chunks,)),
        ],
        input_output_aliases={1: 0} if extra else {},
        cost_estimate=pl.CostEstimate(flops=0, bytes_accessed=4 * tile * pairs * orbitals, transcendentals=0),
        compiler_params=pltpu.CompilerParams(vmem_limit_bytes=GRANT),
        name="turn",
    )(amplitudes, *extra)


def ladder_kernel(order_ref, *refs, pieces, slots):
    piece_refs = refs[:pieces]
    amp_ref, chol_ref, keep_ref, send_ref, window, amps, chols, half, total, amp_came, chol_came = refs[pieces:]
    own = piece_refs[0].shape[1]
    steps, pairs, _ = amp_ref.shape

    def fetch(at, slot):
        return (
            pltpu.make_async_copy(amp_ref.at[at], amps.at[slot], amp_came.at[slot]),
            pltpu.make_async_copy(chol_ref.at[at], chols.at[slot], chol_came.at[slot]),
        )

    def issue(after, upto):
        for c in range(after, min(upto, steps)):
            for copy in fetch(c, c % slots):
                copy.start()
        return max(after, min(upto, steps))

    issued = issue(0, min(slots, 3))
    for i in range(pieces):
        start = pl.multiple_of(order_ref[i] * own, own)
        for a in range(A_WIN):
            window[a, pl.ds(start, own), :] = piece_refs[i][a]

    first, size = 0, 1
    while first < steps:
        here = range(first, min(first + size, steps))
        for c in here:
            for copy in fetch(c, c % slots):
                copy.wait()
        issued = issue(issued, first + slots)
        for c in here:
            for a in range(A_WIN):
                half[c % 2, a * pairs : (a + 1) * pairs, :] = jnp.dot(
                    amps[c % slots], window[a], preferred_element_type=jnp.float32
                ).astype(half.dtype)
            added = jnp.dot(half[c % 2], chols[c % slots], preferred_element_type=jnp.float32)
            total[...] = total[...] + added if c else added
        first += size
        size = min(GROUP, first)

    core = order_ref[pieces]
    chips, _, width, _ = keep_ref.shape
    for a in range(A_WIN):
        turned = jnp.transpose(total[a * pairs : (a + 1) * pairs, :])
        total_t = turned.reshape(chips, CORES, width, pairs)
        first, second = total_t[:, 0], total_t[:, 1]
        keep_ref[:, a] = jnp.where(core == 0, first, second)
        send_ref[:, a] = jnp.where(core == 0, second, first)


def ladder_of(order, pieces, amplitudes, cholesky, chips):
    steps, pairs, orbitals = amplitudes.shape
    _, depth, _ = cholesky.shape
    slots = min(SLOTS, steps)
    width = orbitals // (chips * CORES)
    shape = jax.ShapeDtypeStruct((chips, A_WIN, width, pairs), jnp.float32)
    flops = 2 * steps * pairs * A_WIN * orbitals * depth * 2
    kind = amplitudes.dtype
    return pl.pallas_call(
        functools.partial(ladder_kernel, pieces=len(pieces), slots=slots),
        out_shape=(shape, shape),
        in_specs=[pl.BlockSpec(memory_space=pltpu.SMEM)]
        + [pl.BlockSpec(memory_space=pltpu.VMEM)] * len(pieces)
        + [pl.BlockSpec(memory_space=pltpu.HBM)] * 2,
        out_specs=[pl.BlockSpec(memory_space=pltpu.VMEM)] * 2,
        scratch_shapes=[
            pltpu.VMEM((A_WIN, orbitals, depth), kind),
            pltpu.VMEM((slots, pairs, orbitals), kind),
            pltpu.VMEM((slots, depth, orbitals), kind),
            pltpu.VMEM((2, A_WIN * pairs, depth), kind),
            pltpu.VMEM((A_WIN * pairs, orbitals), jnp.float32),
            pltpu.SemaphoreType.DMA((slots,)),
            pltpu.SemaphoreType.DMA((slots,)),
        ],
        cost_estimate=pl.CostEstimate(
            flops=flops, bytes_accessed=2 * (cholesky.size + amplitudes.size), transcendentals=0
        ),
        compiler_params=pltpu.CompilerParams(vmem_limit_bytes=GRANT),
        name="ladder",
    )(order, *pieces, amplitudes, cholesky)


def shards(cholesky, amplitudes, *, devices):
    return part(cholesky, amplitudes, devices)


def part(cholesky, amplitudes, devices):
    chips = devices // CORES
    ring = ring_order(chips)
    place = [ring.index(chip) for chip in range(chips)]
    me = lax.axis_index("col")
    core = me % CORES

    def along(step):
        return [
            (ring[i] * CORES + c, ring[(i + step) % chips] * CORES + c) for i in range(chips) for c in range(CORES)
        ]

    partner = [(i, i ^ 1) for i in range(devices)]
    window = window_of(cholesky)

    def hop(piece, step):
        return lax.ppermute(piece, "col", along(step))

    mine = [(0, window)]
    ahead = back = window
    by_step = None
    hops = chips // 2
    for at_hop in range(1, hops + 1):
        ahead = hop(ahead, 1)
        mine.append((-at_hop, ahead))
        if at_hop < hops:
            back = hop(back, -1)
            mine.append((at_hop, back))
        by_step = turn(amplitudes, at_hop - 1, hops, by_step)
    theirs = [(far, lax.ppermute(piece, "col", partner)) for far, piece in mine]

    at = sum(jnp.where(me // CORES == chip, place[chip], 0) for chip in range(chips))

    def owner(away):
        where = (at + away) % chips
        return sum(jnp.where(where == i, ring[i], 0) for i in range(chips))

    order = jnp.stack(
        [owner(far) * CORES + core for far, _ in mine]
        + [owner(far) * CORES + 1 - core for far, _ in theirs]
        + [core]
    ).astype(jnp.int32)
    pieces = [piece for _, piece in mine + theirs]
    keep, send = ladder_of(order, pieces, by_step, cholesky, chips)
    summed = keep + lax.ppermute(send, "col", partner)
    groups = [[chip * CORES + c for chip in range(chips)] for c in range(CORES)]
    parts = lax.all_to_all(summed.astype(jnp.bfloat16), "col", 0, 0, tiled=True, axis_index_groups=groups)
    mine_at = lax.broadcasted_iota(jnp.int32, (chips, 1, 1, 1), 0) == me // CORES
    ladder = jnp.where(mine_at, summed, parts.astype(jnp.float32)).sum(0)
    return jnp.transpose(ladder, (2, 0, 1))


def solution(mesh):
    in_specs = (P(("ga", "col"), None, None), P("ga", "col", None))
    out_specs = P("ga", None, "col")
    devices = mesh.shape["col"]
    body = functools.partial(shards, devices=devices)
    return jax.shard_map(body, mesh=mesh, in_specs=in_specs, out_specs=out_specs, check_vma=False)
```
